256 devices in a mesh: row: 32 (over x, y, core), col: 8 (over z).
Axes of the slice: x: 4, y: 4, z: 8, core: 2. Of those that a mesh axis runs over, the one named last changes fastest.
Arguments:
- slab: float32 [16384, 10240], P('row', 'col'), may hold values from -6 to 6
- leaf_y: float32 [16384, 256], P('row', 'col'), may hold values from -0.25 to 0.25
- leaf_t: float32 [8192, 256], P('row', 'col'), may hold values from -0.2 to 2.3, as said below
- tree_y: float32 [5, 8192, 256], P(None, 'row'), may hold values from -0.25 to 0.25
- tree_t: float32 [5, 8192, 256], P(None, 'row'), may hold values from -0.2 to 2.3, as said below
Outputs:
- result: float32 [16384, 10240], P('row', 'col')
The draws below stay inside these ranges and needn't reach their ends.
Inputs may be any that keep to these rules, and one draw needn't show every extreme that they name: `leaf_t`: each 256 x 256 block is upper triangular, with diagonal entries between 1.7 and 2.3 and off-diagonal entries of magnitude at most 0.2. `tree_t`: each 256 x 256 block is upper triangular, with diagonal entries between 1.7 and 2.3 and off-diagonal entries of magnitude at most 0.2; blocks of a section s that do not belong to a node's lower member are not used.
All inputs are finite; a program needn't handle non-finite values.
Results may differ from the reference program's by a relative error of at most 0.0002.
Values sent between devices are 32-bit elements; how exact they have to be, the bound alone decides.
No kernel may reach another device: no remote copies, remote signals or barrier semaphores. Data moves between devices by JAX's collectives and lax.ppermute only.
A program may use at most 64 MiB of HBM per device.

```python
import math
import jax
import jax.numpy as jnp
from jax import lax

B = 256
NCOL = 10240
ROWS_DEV = 512
SECTIONS = 5
M = 16384
N_ROW = 32


def triangle(key, count, low_end, high_end, spread):
    first, second = jax.random.split(jax.random.fold_in(key, 17))
    diag_vals = jax.random.uniform(first, (count * B, B), jnp.float32, low_end, high_end)
    off_vals = jnp.clip(jax.random.normal(second, (count * B, B), jnp.float32) * spread / math.sqrt(B), -0.2, 0.2)
    row_pos = jnp.arange(count * B) % B
    col_pos = jnp.arange(B)
    upper = col_pos[None, :] > row_pos[:, None]
    same = col_pos[None, :] == row_pos[:, None]
    return jnp.where(same, diag_vals, jnp.where(upper, off_vals, 0.0))


def draw_leaf_t(key, part):
    return triangle(key, N_ROW, 1.8, 2.2, 0.4)


def draw_tree_t(key, part):
    values = triangle(key, SECTIONS * N_ROW, 1.8, 2.2, 0.4)
    return values.reshape(SECTIONS, N_ROW * B, B)


def shard_levels(own_key, shape, shards, least, largest):
    level, own = 1.0, jax.random.fold_in(own_key, 6)
    for position, shards_of in shards:
        draws = jnp.exp(jax.random.uniform(jax.random.fold_in(own, position), (shards_of,), jnp.float32, least / len(shards), largest / len(shards)))
        level = level * jnp.repeat(draws, shape[position] // shards_of).reshape([-1 if axis == position else 1 for axis in range(len(shape))])
    return level


def noise(rng, extent, width, bound, pieces=(), dtype=jnp.bfloat16):
    values = jax.random.normal(rng, extent, jnp.float32) * width
    if len(pieces) > 0:
        values = shard_levels(rng, extent, pieces, -0.22, 0.18) * values
    return jnp.clip(values, min=-bound, max=bound).astype(dtype)


def setup_inputs(seed: int = 0) -> dict:
    splits = jax.random.split(jax.random.key(seed), 6)
    return {
        "slab": noise(splits[0], (M, NCOL), 1.0, 6.0, ((0, 32), (1, 8)), jnp.float32),
        "leaf_y": noise(splits[1], (M, B), ROWS_DEV ** -0.5, 0.25, ((0, 32), (1, 8)), jnp.float32),
        "leaf_t": draw_leaf_t(jax.random.fold_in(splits[5], 71), 0),
        "tree_y": noise(splits[3], (SECTIONS, N_ROW * B, B), (2 * B) ** -0.5, 0.25, ((1, 32),), jnp.float32),
        "tree_t": draw_tree_t(jax.random.fold_in(splits[5], 71), 0),
    }


def contract(left, right):
    return lax.dot_general(left, right, (((0,), (0,)), ((), ())), precision=lax.Precision.HIGHEST, preferred_element_type=jnp.float32)


def reflect(vectors, factor, block):
    coeffs = contract(vectors, block)
    scaled = contract(factor, coeffs)
    return block - jnp.dot(vectors, scaled, precision=lax.Precision.HIGHEST, preferred_element_type=jnp.float32)


def reference(slab, leaf_y, leaf_t, tree_y, tree_t):
    blocks = slab.reshape(N_ROW, ROWS_DEV, NCOL)
    vectors = leaf_y.reshape(N_ROW, ROWS_DEV, B)
    factors = leaf_t.reshape(N_ROW, B, B)
    updated = lax.map(lambda trio: reflect(trio[0], trio[1], trio[2]), (vectors, factors, blocks))
    heads = updated[:, :B, :]
    for section in range(SECTIONS):
        stride = 2 ** section
        groups = N_ROW // (2 * stride)
        grouped = heads.reshape(groups, 2, stride, B, NCOL)
        first_rows = grouped[:, 0, 0]
        second_rows = grouped[:, 1, 0]
        node_y = tree_y[section].reshape(groups, 2, stride, B, B)
        first_y = node_y[:, 0, 0]
        second_y = node_y[:, 1, 0]
        node_t = tree_t[section].reshape(groups, 2, stride, B, B)[:, 0, 0]
        coeffs = jnp.einsum("grb,grc->gbc", first_y, first_rows, precision=lax.Precision.HIGHEST)
        coeffs = coeffs + jnp.einsum("grb,grc->gbc", second_y, second_rows, precision=lax.Precision.HIGHEST)
        scaled = jnp.einsum("gbk,gbc->gkc", node_t, coeffs, precision=lax.Precision.HIGHEST)
        first_rows = first_rows - jnp.einsum("grk,gkc->grc", first_y, scaled, precision=lax.Precision.HIGHEST)
        second_rows = second_rows - jnp.einsum("grk,gkc->grc", second_y, scaled, precision=lax.Precision.HIGHEST)
        grouped = grouped.at[:, 0, 0].set(first_rows).at[:, 1, 0].set(second_rows)
        heads = grouped.reshape(N_ROW, B, NCOL)
    result = jnp.concatenate([heads, updated[:, B:, :]], axis=1)
    return result.reshape(M, NCOL)
```

```python
import jax
import jax.numpy as jnp
from jax import lax
from jax.sharding import PartitionSpec as P


ROWS = 32
COLS = 8


def dot(left, right, dims):
    return lax.dot_general(
        left,
        right,
        ((dims[0], dims[1]), ((), ())),
        precision=lax.Precision.HIGH,
        preferred_element_type=jnp.float32,
    )


def ring(block, step):
    return lax.ppermute(block, "col", [(i, (i + step) % COLS) for i in range(COLS)])


def gathered(own):
    from_below = ring(own, 1)
    from_above = ring(own, -1)
    two_below = ring(own, 2)
    two_above = ring(own, -2)
    three_below = ring(two_below, 1)
    three_above = ring(two_above, -1)
    opposite = ring(two_below, 2)
    turned = jnp.concatenate(
        [own, from_above, two_above, three_above, opposite, three_below, two_below, from_below], axis=0
    )
    length = turned.shape[0]
    start = length - lax.axis_index("col") * own.shape[0]
    return lax.dynamic_slice_in_dim(jnp.concatenate([turned, turned], axis=0), start, length, axis=0)


def pairs(section):
    stride = 2**section
    return [
        (low, low + stride)
        for base in range(0, ROWS, 2 * stride)
        for low in ((base, base + 1) if section else (base,))
    ]


def both(routes):
    return routes + [(high, low) for low, high in routes]


def shards(slab, leaf_y, leaf_t, tree_y, tree_t):
    width = leaf_t.shape[0]
    rows = leaf_y.shape[0]
    half = slab.shape[1] // 2
    position = lax.axis_index("row")
    first_core = position % 2 == 0
    core_pairs = pairs(0)
    other_y = lax.ppermute(tree_y, "row", both(core_pairs))
    other_t = lax.ppermute(tree_t, "row", both(core_pairs))
    full = gathered(jnp.concatenate([leaf_y.T, leaf_t.T], axis=1))
    leaf_rows = full[:, :rows]
    leaf_tri = full[:, rows:]
    coeffs = dot(leaf_rows, slab, ((1,), (0,)))
    scaled = dot(leaf_tri, coeffs, ((1,), (0,)))
    updated = slab - dot(leaf_rows, scaled, ((0,), (0,)))
    top = updated[:width]
    tail = updated[width:]
    left, right = top[:, :half], top[:, half:]
    mine = jnp.where(first_core, left, right)
    theirs = lax.ppermute(jnp.where(first_core, right, left), "row", both(core_pairs))
    factor = jnp.where(first_core, tree_t[0], other_t[0])
    node = dot(tree_y[0], mine, ((0,), (0,))) + dot(other_y[0], theirs, ((0,), (0,)))
    node = dot(factor, node, ((0,), (0,)))
    mine = mine - dot(tree_y[0], node, ((1,), (0,)))
    theirs = theirs - dot(other_y[0], node, ((1,), (0,)))
    returned = lax.ppermute(theirs, "row", core_pairs)
    rest = jnp.where(first_core, mine, theirs)
    for section in range(1, tree_y.shape[0]):
        stride = 2**section
        routes = pairs(section)
        vectors = jnp.where(first_core, tree_y[section], other_y[section])
        factor = jnp.where(first_core, tree_t[section], other_t[section])
        chip_row = position - position % 2
        is_low = chip_row % (2 * stride) == 0
        active = chip_row % stride == 0
        factor = jnp.where(is_low, factor, lax.ppermute(factor, "row", routes))
        part = dot(vectors, rest, ((0,), (0,)))
        part = part + lax.ppermute(part, "row", both(routes))
        node = dot(factor, part, ((0,), (0,)))
        rest = jnp.where(active, rest - dot(vectors, node, ((1,), (0,))), rest)
    final = lax.ppermute(rest, "row", [(high, low) for low, high in core_pairs])
    head = jnp.where(
        first_core,
        jnp.concatenate([rest, final], axis=1),
        jnp.concatenate([returned, mine], axis=1),
    )
    return jnp.concatenate([head, tail], axis=0)


def solution(mesh):
    in_specs = (
        P("row", "col"),
        P("row", "col"),
        P("row", "col"),
        P(None, "row", None),
        P(None, "row", None),
    )
    out_specs = P("row", "col")
    return jax.shard_map(shards, mesh=mesh, in_specs=in_specs, out_specs=out_specs, check_vma=False)
```

```python
import functools

import jax
import jax.numpy as jnp
from jax import lax
from jax.experimental import pallas as pl
from jax.experimental.pallas import tpu as pltpu
from jax.sharding import PartitionSpec as P


ROWS = 32
COLS = 8
B = 256
HALF = 640
CHUNKS = ((0, 384), (384, 256))
F32 = jnp.float32
BF16 = jnp.bfloat16
VMEM = pl.BlockSpec(memory_space=pltpu.VMEM)
SMEM = pl.BlockSpec(memory_space=pltpu.SMEM)
ANY = pl.BlockSpec(memory_space=pl.ANY)
PARAMS = pltpu.CompilerParams(vmem_limit_bytes=16 << 20)


def struct(shape, dtype=F32):
    return jax.ShapeDtypeStruct(shape, dtype)


def near(shape, dtype=F32):
    return pltpu.VMEM(shape, dtype)


def here(*values):
    return tuple(pltpu.with_memory_space_constraint(value, pltpu.VMEM) for value in values)


def cost(flops, moved):
    return pl.CostEstimate(flops=flops, bytes_accessed=moved, transcendentals=0)


def split(value):
    high = value.astype(BF16)
    return high, (value - high.astype(F32)).astype(BF16)


def dot3(left, right):
    one = functools.partial(jnp.dot, preferred_element_type=F32)
    return one(left[0], right[0]) + (one(left[0], right[1]) + one(left[1], right[0]))


def leaf_top(slab, mats, out_mine, out_send, out_z, core, width):
    y_rows, y_top, tri = mats
    coeffs = dot3(y_rows, split(slab))
    scaled = split(dot3(tri, split(coeffs)))
    out_z[0] = scaled[0]
    out_z[1] = scaled[1]
    top = slab[:B] - dot3(y_top, scaled)
    left, right = top[:, :width], top[:, width:]
    out_mine[...] = jnp.where(core == 0, left, right)
    out_send[...] = jnp.where(core == 0, right, left)


def load(slab, buf, sem, start, width):
    return [
        pltpu.make_async_copy(
            slab.at[:, pl.ds(side * HALF + start, width)], buf.at[:, pl.ds(side * width, width)], sem.at[side]
        )
        for side in range(2)
    ]


def leaf_first(start, width, ids, *refs):
    pieces = refs[:COLS]
    slab, out_mine, out_send, out_z, out_rows, out_y, out_tri, buf, full, sem = refs[COLS:]
    copies = load(slab, buf, sem, start, width)
    for copy in copies:
        copy.start()
    core, place = ids[0], ids[1]
    count = pieces[0].shape[0]
    for step in range(COLS):
        row = pl.multiple_of(lax.rem(place + step, COLS) * count, count)
        full[pl.ds(row, count), :] = pieces[step][...]
    y_rows = full[:, : 2 * B]
    rows = split(y_rows)
    out_rows[0] = rows[0]
    out_rows[1] = rows[1]
    tri = split(full[:, 2 * B :])
    out_tri[0] = tri[0]
    out_tri[1] = tri[1]
    turned = split(y_rows.T)
    out_y[0] = turned[0]
    out_y[1] = turned[1]
    y_top = (turned[0][:B], turned[1][:B])
    for copy in copies:
        copy.wait()
    leaf_top(buf[...], (rows, y_top, tri), out_mine, out_send, out_z, core, width)


def leaf_second(start, width, ids, slab, rows, y, tri, out_mine, out_send, out_z, buf, sem):
    copies = load(slab, buf, sem, start, width)
    for copy in copies:
        copy.start()
    for copy in copies:
        copy.wait()
    mats = ((rows[0], rows[1]), (y[0, :B], y[1, :B]), (tri[0], tri[1]))
    leaf_top(buf[...], mats, out_mine, out_send, out_z, ids[0], width)


def leaf_bottom(slab, y, z_one, z_two, out, buf, result, sem):
    width = 2 * HALF
    get = pltpu.make_async_copy(slab.at[pl.ds(B, B), :], buf, sem.at[0])
    get.start()
    get.wait()
    low = (y[0, B:], y[1, B:])
    for (start, size), z in zip(CHUNKS, (z_one, z_two)):
        change = dot3(low, (z[0], z[1]))
        for side in range(2):
            at = side * HALF + start
            result[:, at : at + size] = buf[:, at : at + size] - change[:, side * size : (side + 1) * size]
    put = pltpu.make_async_copy(result, out.at[pl.ds(B, B), :], sem.at[1])
    put.start()
    put.wait()


def keep(out, place, pair):
    out[place] = pair[0]
    out[place + 1] = pair[1]


def prepare_first(ids, own_y, other_y, own_t, other_t, out):
    keep(out, 0, split(own_y[0].T))
    keep(out, 2, split(other_y[0].T))
    keep(out, 4, split(own_y[0]))
    keep(out, 6, split(other_y[0]))
    keep(out, 8, split(jnp.where(ids[0] == 0, own_t[0], other_t[0]).T))


def prepare(ids, own_y, other_y, factor, out):
    vectors = jnp.where(ids[0] == 0, own_y[0], other_y[0])
    keep(out, 0, split(vectors.T))
    keep(out, 2, split(vectors))
    keep(out, 4, split(factor[...].T))


def section_first(ids, mine, theirs, mats, following, out_rest, out_done, out_part):
    at = lambda place: (mats[place], mats[place + 1])
    own, other = mine[...], theirs[...]
    node = dot3(at(0), split(own)) + dot3(at(2), split(other))
    node = split(dot3(at(8), split(node)))
    own = own - dot3(at(4), node)
    other = other - dot3(at(6), node)
    rest = jnp.where(ids[0] == 0, own, other)
    out_rest[...] = rest
    out_done[...] = jnp.where(ids[0] == 0, other, own)
    out_part[...] = dot3((following[0], following[1]), split(rest))


def update(active, part, other, rest, mats):
    node = split(dot3((mats[4], mats[5]), split(part[...] + other[...])))
    change = dot3((mats[2], mats[3]), node)
    return rest[...] - jnp.where(active != 0, change, 0.0)


def section_next(place, ids, part, other, rest, mats, following, out_rest, out_part):
    new = update(ids[place], part, other, rest, mats)
    out_rest[...] = new
    out_part[...] = dot3((following[0], following[1]), split(new))


def section_last(place, ids, part, other, rest, mats, done, out_keep, out_send):
    new = update(ids[place], part, other, rest, mats)
    out_keep[...] = jnp.where(ids[0] == 0, new, done[...])
    out_send[...] = jnp.where(ids[0] == 0, done[...], new)


def finish(ids, keep_one, keep_two, got_one, got_two, _, out, sem):
    for core in range(2):

        @pl.when(ids[0] == core)
        def _():
            copies = []
            for number, ((start, size), kept, got) in enumerate(
                zip(CHUNKS, (keep_one, keep_two), (got_one, got_two))
            ):
                for side, source in ((core, kept), (1 - core, got)):
                    copies.append(
                        pltpu.make_async_copy(
                            source,
                            out.at[pl.ds(0, B), pl.ds(side * HALF + start, size)],
                            sem.at[2 * number + (side == core)],
                        )
                    )
            for copy in copies:
                copy.start()
            for copy in copies:
                copy.wait()


def ring(block, step):
    return lax.ppermute(block, "col", [(i, (i + step) % COLS) for i in range(COLS)])


def pieces_of(own):
    two_below = ring(own, 2)
    two_above = ring(own, -2)
    from_below = ring(own, 1)
    from_above = ring(own, -1)
    opposite = ring(two_below, 2)
    three_below = ring(two_below, 1)
    three_above = ring(two_above, -1)
    return [own, from_above, two_above, three_above, opposite, three_below, two_below, from_below]


def pairs(section):
    stride = 2**section
    return [
        (low, low + stride)
        for base in range(0, ROWS, 2 * stride)
        for low in ((base, base + 1) if section else (base,))
    ]


def both(routes):
    return routes + [(high, low) for low, high in routes]


def shards(slab, leaf_y, leaf_t, tree_y, tree_t):
    position = lax.axis_index("row")
    core = position % 2
    chip_row = position - core
    place = lax.axis_index("col")
    sections = tree_y.shape[0]
    active = [(chip_row % 2**section == 0).astype(jnp.int32) for section in range(sections)]
    ids = jnp.stack([core.astype(jnp.int32), place.astype(jnp.int32)] + active)
    core_pairs = both(pairs(0))

    pieces = pieces_of(jnp.concatenate([leaf_y.T, leaf_t.T], axis=1))
    other_y = lax.ppermute(tree_y, "row", core_pairs)
    other_t = lax.ppermute(tree_t, "row", core_pairs)

    factors = [None]
    for section in range(1, sections):
        own = jnp.where(core == 0, tree_t[section], other_t[section])
        sent = lax.ppermute(own, "row", pairs(section))
        factors.append(jnp.where(chip_row % (2 * 2**section) == 0, own, sent))

    block = lambda section: pl.BlockSpec((1, B, B), lambda i: (section, 0, 0))
    mats = [
        pl.pallas_call(
            prepare_first,
            grid=(1,),
            out_shape=near((10, B, B), BF16),
            in_specs=[SMEM, block(0), block(0), block(0), block(0)],
            out_specs=pl.BlockSpec((10, B, B), lambda i: (0, 0, 0)),
            compiler_params=PARAMS,
            cost_estimate=cost(2 * 10**8, 2 * 10**6),
        )(ids, tree_y, other_y, tree_t, other_t)
    ]
    for section in range(1, sections):
        mats.append(
            pl.pallas_call(
                prepare,
                grid=(1,),
                out_shape=near((6, B, B), BF16),
                in_specs=[SMEM, block(section), block(section), pl.BlockSpec((B, B), lambda i: (0, 0))],
                out_specs=pl.BlockSpec((6, B, B), lambda i: (0, 0, 0)),
                compiler_params=PARAMS,
                cost_estimate=cost(2 * 10**8, 2 * 10**6),
            )(ids, tree_y, other_y, factors[section])
        )

    (start, size), (start_two, size_two) = CHUNKS
    rows = slab.shape[0]
    leaf_out = lambda width: (near((B, width)), near((B, width)), near((2, B, 2 * width), BF16))
    mine_one, send_one, z_one, y_rows, y_cols, tri = pl.pallas_call(
        functools.partial(leaf_first, start, size),
        out_shape=leaf_out(size)
        + (near((2, B, rows), BF16), near((2, rows, B), BF16), near((2, B, B), BF16)),
        in_specs=[SMEM] + [VMEM] * COLS + [ANY],
        out_specs=(VMEM,) * 6,
        scratch_shapes=[
            pltpu.VMEM((rows, 2 * size), F32),
            pltpu.VMEM((B, rows + B), F32),
            pltpu.SemaphoreType.DMA((2,)),
        ],
        compiler_params=PARAMS,
        cost_estimate=cost(3 * 10**9, 4 * 10**6),
    )(ids, *here(*pieces), slab)
    got_one = lax.ppermute(send_one, "row", core_pairs)
    mine_two, send_two, z_two = pl.pallas_call(
        functools.partial(leaf_second, start_two, size_two),
        out_shape=leaf_out(size_two),
        in_specs=[SMEM, ANY, VMEM, VMEM, VMEM],
        out_specs=(VMEM,) * 3,
        scratch_shapes=[pltpu.VMEM((rows, 2 * size_two), F32), pltpu.SemaphoreType.DMA((2,))],
        compiler_params=PARAMS,
        cost_estimate=cost(2 * 10**9, 3 * 10**6),
    )(ids, slab, *here(y_rows, y_cols, tri))
    got_two = lax.ppermute(send_two, "row", core_pairs)
    result = pl.pallas_call(
        leaf_bottom,
        out_shape=struct(slab.shape),
        in_specs=[ANY, VMEM, VMEM, VMEM],
        out_specs=ANY,
        scratch_shapes=[
            pltpu.VMEM((B, 2 * HALF), F32),
            pltpu.VMEM((B, 2 * HALF), F32),
            pltpu.SemaphoreType.DMA((2,)),
        ],
        compiler_params=PARAMS,
        cost_estimate=cost(2 * 10**9, 4 * 10**6),
    )(slab, *here(y_cols, z_one, z_two))

    state = []
    for (_, width), mine, theirs in zip(CHUNKS, (mine_one, mine_two), (got_one, got_two)):
        shape = near((B, width))
        state.append(
            pl.pallas_call(
                section_first,
                out_shape=(shape, shape, shape),
                in_specs=[SMEM] + [VMEM] * 4,
                out_specs=(VMEM,) * 3,
                compiler_params=PARAMS,
                cost_estimate=cost(10**9, 3 * 10**6),
            )(ids, *here(mine, theirs, mats[0], mats[1]))
        )
    for section in range(1, sections):
        routes = both(pairs(section))
        last = section == sections - 1
        for number, (_, width) in enumerate(CHUNKS):
            rest, done, part = state[number]
            other = lax.ppermute(part, "row", routes)
            shape = near((B, width))
            body = section_last if last else section_next
            one, two = pl.pallas_call(
                functools.partial(body, 2 + section),
                out_shape=(shape, shape),
                in_specs=[SMEM] + [VMEM] * 5,
                out_specs=(VMEM,) * 2,
                compiler_params=PARAMS,
                cost_estimate=cost(10**9, 3 * 10**6),
            )(ids, *here(part, other, rest, mats[section], done if last else mats[section + 1]))
            state[number] = (one, done, two)
    kept = [entry[0] for entry in state]
    got = [lax.ppermute(entry[2], "row", core_pairs) for entry in state]
    return pl.pallas_call(
        finish,
        out_shape=struct(slab.shape),
        in_specs=[SMEM] + [VMEM] * 4 + [ANY],
        out_specs=ANY,
        input_output_aliases={5: 0},
        scratch_shapes=[pltpu.SemaphoreType.DMA((4,))],
        compiler_params=PARAMS,
        cost_estimate=cost(10**6, 3 * 10**6),
    )(ids, *here(*kept, *got), result)


def solution(mesh):
    in_specs = (
        P("row", "col"),
        P("row", "col"),
        P("row", "col"),
        P(None, "row", None),
        P(None, "row", None),
    )
    out_specs = P("row", "col")
    return jax.shard_map(shards, mesh=mesh, in_specs=in_specs, out_specs=out_specs, check_vma=False)
```

```python
import functools

import jax
import jax.numpy as jnp
from jax import lax
from jax.experimental import pallas as pl
from jax.experimental.pallas import tpu as pltpu
from jax.sharding import PartitionSpec as P


ROWS = 32
COLS = 8
LAST = 4
B = 256
HALF = 640
CHUNKS = ((0, 384), (384, 256))


F32 = jnp.float32
BF16 = jnp.bfloat16
VMEM = pl.BlockSpec(memory_space=pltpu.VMEM)
HBM = pl.BlockSpec(memory_space=pltpu.HBM)
PARAMS = pltpu.CompilerParams(vmem_limit_bytes=16 << 20)


def struct(shape, dtype=F32):
    return jax.ShapeDtypeStruct(shape, dtype)


def core_index():
    return lax.rem(lax.axis_index("row"), 2)


def is_member(section):
    row = lax.axis_index("row")
    return lax.rem(row - lax.rem(row, 2), 2**section) == 0


def is_low(section):
    return is_member(section + 1)


def near(shape, dtype=F32):
    return pltpu.VMEM(shape, dtype)


def here(*values):
    return tuple(pltpu.with_memory_space_constraint(value, pltpu.VMEM) for value in values)


def away(*values):
    return tuple(pltpu.with_memory_space_constraint(value, pltpu.HBM) for value in values)


def cost(flops, moved):
    return pl.CostEstimate(flops=flops, bytes_accessed=moved, transcendentals=0)


def split(value):
    high = value.astype(BF16)
    return high, (value - high.astype(F32)).astype(BF16)


def dot3(left, right):
    one = functools.partial(jnp.dot, preferred_element_type=F32)
    return one(left[0], right[0]) + (one(left[0], right[1]) + one(left[1], right[0]))


def leaf_top(slab, mats, out_mine, out_send, out_z, core, width):
    y_rows, y_top, tri = mats
    coeffs = dot3(y_rows, split(slab))
    scaled = split(dot3(tri, split(coeffs)))
    out_z[0] = scaled[0]
    out_z[1] = scaled[1]
    top = slab[:B] - dot3(y_top, scaled)
    left, right = top[:, :width], top[:, width:]
    out_mine[...] = jnp.where(core == 0, left, right)
    out_send[...] = jnp.where(core == 0, right, left)


def load(slab, buf, sem, start, width):
    return [
        pltpu.make_async_copy(
            slab.at[:, pl.ds(side * HALF + start, width)], buf.at[:, pl.ds(side * width, width)], sem.at[side]
        )
        for side in range(2)
    ]


def leaf_first(start, width, *refs):
    pieces = refs[:COLS]
    slab, out_mine, out_send, out_z, out_rows, out_y, out_tri, buf, full, sem = refs[COLS:]
    copies = load(slab, buf, sem, start, width)
    for copy in copies:
        copy.start()
    core, place = core_index(), lax.axis_index("col")
    count = pieces[0].shape[0]
    for step in range(COLS):
        row = pl.multiple_of(lax.rem(place + step, COLS) * count, count)
        full[pl.ds(row, count), :] = pieces[step][...]
    y_rows = full[:, : 2 * B]
    rows = split(y_rows)
    out_rows[0] = rows[0]
    out_rows[1] = rows[1]
    tri = split(full[:, 2 * B :])
    out_tri[0] = tri[0]
    out_tri[1] = tri[1]
    turned = split(y_rows.T)
    out_y[0] = turned[0]
    out_y[1] = turned[1]
    y_top = (turned[0][:B], turned[1][:B])
    for copy in copies:
        copy.wait()
    leaf_top(buf[...], (rows, y_top, tri), out_mine, out_send, out_z, core, width)


def leaf_second(start, width, slab, rows, y, tri, out_mine, out_send, out_z, buf, sem):
    copies = load(slab, buf, sem, start, width)
    for copy in copies:
        copy.start()
    for copy in copies:
        copy.wait()
    mats = ((rows[0], rows[1]), (y[0, :B], y[1, :B]), (tri[0], tri[1]))
    leaf_top(buf[...], mats, out_mine, out_send, out_z, core_index(), width)


def leaf_bottom(slab, y, *refs):
    count = len(CHUNKS)
    scaled, (out, buf, result, sem) = refs[:count], refs[count:]
    get = pltpu.make_async_copy(slab.at[pl.ds(B, B), :], buf, sem.at[0])
    get.start()
    get.wait()
    low = (y[0, B:], y[1, B:])
    for (start, size), z in zip(CHUNKS, scaled):
        change = dot3(low, (z[0], z[1]))
        for side in range(2):
            at = side * HALF + start
            result[:, at : at + size] = buf[:, at : at + size] - change[:, side * size : (side + 1) * size]
    put = pltpu.make_async_copy(result, out.at[pl.ds(B, B), :], sem.at[1])
    put.start()
    put.wait()


def keep(out, place, pair):
    out[place] = pair[0]
    out[place + 1] = pair[1]


def prepare_first(own_y, own_t, other_y, other_t, out):
    keep(out, 0, split(own_y[0].T))
    keep(out, 2, split(other_y[0].T))
    keep(out, 4, split(own_y[0]))
    keep(out, 6, split(other_y[0]))
    keep(out, 8, split(jnp.where(core_index() == 0, own_t[0], other_t[0]).T))


def prepare(section, own_y, other_y, out):
    vectors = jnp.where(core_index() == 0, own_y[0], other_y[section])
    keep(out, 0, split(vectors.T))
    keep(out, 2, split(vectors))


def prepare_factors(first, own_t, other_t, got, sent, out):
    upper = got[...] + sent[...]
    for number in range(2):
        own = jnp.where(core_index() == 0, own_t[first + number], other_t[first + number])
        keep(out, 2 * number, split(jnp.where(is_low(first + number), own, upper).T))


def section_first(mine, theirs, mats, following, out_rest, out_done, out_part):
    at = lambda place: (mats[place], mats[place + 1])
    own, other = mine[...], theirs[...]
    node = dot3(at(0), split(own)) + dot3(at(2), split(other))
    node = split(dot3(at(8), split(node)))
    own = own - dot3(at(4), node)
    other = other - dot3(at(6), node)
    rest = jnp.where(core_index() == 0, own, other)
    out_rest[...] = rest
    out_done[...] = jnp.where(core_index() == 0, other, own)
    out_part[...] = dot3((following[0], following[1]), split(rest))


def update(section, part, other, rest, mats, factor):
    at = 2 * (1 - section % 2)
    node = dot3((factor[at], factor[at + 1]), split(part[...] + other[...]))
    change = dot3((mats[2], mats[3]), split(node))
    return rest[...] - jnp.where(is_member(section), change, 0.0)


def section_next(section, part, other, rest, mats, factor, following, out_rest, out_part):
    new = update(section, part, other, rest, mats, factor)
    out_rest[...] = new
    out_part[...] = dot3((following[0], following[1]), split(new))


def section_last(section, part, other, rest, mats, factor, done, out_keep, out_send):
    new = update(section, part, other, rest, mats, factor)
    out_keep[...] = jnp.where(core_index() == 0, new, done[...])
    out_send[...] = jnp.where(core_index() == 0, done[...], new)


def finish(*refs):
    count = len(CHUNKS)
    kept, got, (_, out, sem) = refs[:count], refs[count : 2 * count], refs[2 * count :]
    for core in range(2):

        @pl.when(core_index() == core)
        def _():
            copies = []
            for number, (start, size) in enumerate(CHUNKS):
                for kind, (side, source) in enumerate(((core, kept[number]), (1 - core, got[number]))):
                    place = out.at[pl.ds(0, B), pl.ds(side * HALF + start, size)]
                    copies.append(pltpu.make_async_copy(source, place, sem.at[2 * number + kind]))
            for copy in copies:
                copy.start()
            for copy in copies:
                copy.wait()


def ring(block, step):
    return lax.ppermute(block, "col", [(i, (i + step) % COLS) for i in range(COLS)])


def pieces_of(own):
    two_below = ring(own, 2)
    two_above = ring(own, -2)
    from_below = ring(own, 1)
    from_above = ring(own, -1)
    opposite = ring(two_below, 2)
    three_below = ring(two_below, 1)
    three_above = ring(two_above, -1)
    return [own, from_above, two_above, three_above, opposite, three_below, two_below, from_below]


def pairs(section):
    stride = 2**section
    return [
        (low, low + stride)
        for base in range(0, ROWS, 2 * stride)
        for low in ((base, base + 1) if section else (base,))
    ]


def both(routes):
    return routes + [(high, low) for low, high in routes]


def call(body, outs, specs, args, scratch=(), flops=10**9, **options):
    return pl.pallas_call(
        body,
        out_shape=outs,
        in_specs=specs,
        out_specs=jax.tree.map(lambda _: HBM if options.get("far") else VMEM, outs),
        scratch_shapes=scratch,
        compiler_params=PARAMS,
        cost_estimate=cost(flops, 3 * 10**6),
        **{key: value for key, value in options.items() if key != "far"},
    )(*args)


def swap(block, routes):
    return lax.ppermute(block, "row", routes)


def shards(slab, leaf_y, leaf_t, tree_y, tree_t):
    core = core_index()
    core_pairs = both(pairs(0))

    pieces = pieces_of(jnp.concatenate([leaf_y.T, leaf_t.T], axis=1))
    other_y = swap(tree_y, core_pairs)
    other_t = swap(tree_t, core_pairs)

    def prepared(body, count, section, own, others):
        block = pl.BlockSpec((1, B, B), lambda i: (section, 0, 0))
        return pl.pallas_call(
            body,
            grid=(1,),
            out_shape=near((count, B, B), BF16),
            in_specs=[block] * len(own) + [VMEM] * len(others),
            out_specs=VMEM,
            compiler_params=PARAMS,
            cost_estimate=cost(2 * 10**8, 2 * 10**6),
        )(*away(*own), *here(*others))

    mats = [prepared(prepare_first, 10, 0, (tree_y, tree_t), (other_y, other_t))]
    for section in range(1, LAST + 1):
        body = functools.partial(prepare, section)
        mats.append(prepared(body, 4, section, (tree_y,), (other_y,)))
    factors = [None]
    for first in (1, 3):
        block = jnp.where(core == 0, tree_t[first], other_t[first + 1])
        routes = [(low, high) for low, high in pairs(first) if low % 2 == 0]
        routes += [(low, high) for low, high in pairs(first + 1) if low % 2 == 1]
        got = swap(block, routes)
        sent = swap(got, core_pairs)
        both_factors = call(
            functools.partial(prepare_factors, first),
            near((4, B, B), BF16),
            [VMEM] * 4,
            here(tree_t, other_t, got, sent),
        )
        factors += [both_factors] * 2

    rows = slab.shape[0]
    state, scaled = [], []
    for number, (start, size) in enumerate(CHUNKS):
        outs = (near((B, size)), near((B, size)), near((2, B, 2 * size), BF16))
        scratch = [pltpu.VMEM((rows, 2 * size), F32), pltpu.SemaphoreType.DMA((2,))]
        if number == 0:
            outs += (near((2, B, rows), BF16), near((2, rows, B), BF16), near((2, B, B), BF16))
            mine, send, z, y_rows, y_cols, tri = call(
                functools.partial(leaf_first, start, size),
                outs,
                [VMEM] * COLS + [HBM],
                here(*pieces) + away(slab),
                scratch[:1] + [pltpu.VMEM((B, rows + B), F32)] + scratch[1:],
            )
        else:
            mine, send, z = call(
                functools.partial(leaf_second, start, size),
                outs,
                [HBM] + [VMEM] * 3,
                away(slab) + here(y_rows, y_cols, tri),
                scratch,
            )
        scaled.append(z)
        theirs = swap(send, core_pairs)
        state.append(
            call(section_first, (near((B, size)),) * 3, [VMEM] * 4, here(mine, theirs, mats[0], mats[1]))
        )
    result = call(
        leaf_bottom,
        struct(slab.shape),
        [HBM] + [VMEM] * (1 + len(CHUNKS)),
        away(slab) + here(y_cols, *scaled),
        [pltpu.VMEM((B, 2 * HALF), F32)] * 2 + [pltpu.SemaphoreType.DMA((2,))],
        far=True,
    )
    for section in range(1, LAST + 1):
        last = section == LAST
        for number, (_, size) in enumerate(CHUNKS):
            rest, done, part = state[number]
            other = swap(part, both(pairs(section)))
            one, two = call(
                functools.partial(section_last if last else section_next, section),
                (near((B, size)),) * 2,
                [VMEM] * 6,
                here(part, other, rest, mats[section], factors[section], done if last else mats[section + 1]),
            )
            state[number] = (one, done, two)
    kept = [entry[0] for entry in state]
    got = [swap(entry[2], core_pairs) for entry in state]
    return call(
        finish,
        struct(slab.shape),
        [VMEM] * (2 * len(CHUNKS)) + [HBM],
        here(*kept, *got) + (result,),
        [pltpu.SemaphoreType.DMA((2 * len(CHUNKS),))],
        far=True,
        input_output_aliases={2 * len(CHUNKS): 0},
    )


def solution(mesh):
    in_specs = (
        P("row", "col"),
        P("row", "col"),
        P("row", "col"),
        P(None, "row", None),
        P(None, "row", None),
    )
    out_specs = P("row", "col")

    return jax.shard_map(shards, mesh=mesh, in_specs=in_specs, out_specs=out_specs, check_vma=False)
```

```python
import functools

import jax
import jax.numpy as jnp
from jax import lax
from jax.experimental import pallas as pl
from jax.experimental.pallas import tpu as pltpu
from jax.sharding import PartitionSpec as P


ROWS = 32
COLS = 8
LAST = 4
B = 256
HALF = 640
CHUNKS = ((0, 384), (384, 256))


F32 = jnp.float32
BF16 = jnp.bfloat16
VMEM = pl.BlockSpec(memory_space=pltpu.VMEM)
HBM = pl.BlockSpec(memory_space=pltpu.HBM)
PARAMS = pltpu.CompilerParams(vmem_limit_bytes=16 << 20)


def struct(shape, dtype=F32):
    return jax.ShapeDtypeStruct(shape, dtype)


def core_index():
    return lax.rem(lax.axis_index("row"), 2)


def is_member(section):
    row = lax.axis_index("row")
    return lax.rem(row - lax.rem(row, 2), 2**section) == 0


def is_low(section):
    return is_member(section + 1)


def near(shape, dtype=F32):
    return pltpu.VMEM(shape, dtype)


def here(*values):
    return tuple(pltpu.with_memory_space_constraint(value, pltpu.VMEM) for value in values)


def away(*values):
    return tuple(pltpu.with_memory_space_constraint(value, pltpu.HBM) for value in values)


def cost(flops, moved):
    return pl.CostEstimate(flops=flops, bytes_accessed=moved, transcendentals=0)


def split(value):
    high = value.astype(BF16)
    return high, (value - high.astype(F32)).astype(BF16)


def dot3(left, right):
    one = functools.partial(jnp.dot, preferred_element_type=F32)
    return one(left[0], right[0]) + (one(left[0], right[1]) + one(left[1], right[0]))


def leaf_top(slab, mats, out_mine, out_send, out_z, core, width):
    y_rows, y_top, tri = mats
    coeffs = dot3(y_rows, split(slab))
    scaled = split(dot3(tri, split(coeffs)))
    out_z[0] = scaled[0]
    out_z[1] = scaled[1]
    top = slab[:B] - dot3(y_top, scaled)
    left, right = top[:, :width], top[:, width:]
    out_mine[...] = jnp.where(core == 0, left, right)
    out_send[...] = jnp.where(core == 0, right, left)


def load(slab, buf, sem, start, width):
    return [
        pltpu.make_async_copy(
            slab.at[:, pl.ds(side * HALF + start, width)], buf.at[:, pl.ds(side * width, width)], sem.at[side]
        )
        for side in range(2)
    ]


def leaf_first(start, width, *refs):
    pieces = refs[:COLS]
    slab, out_mine, out_send, out_z, out_rows, out_y, out_tri, buf, full, sem = refs[COLS:]
    copies = load(slab, buf, sem, start, width)
    for copy in copies:
        copy.start()
    core, place = core_index(), lax.axis_index("col")
    count = pieces[0].shape[0]
    for step in range(COLS):
        row = pl.multiple_of(lax.rem(place + step, COLS) * count, count)
        full[pl.ds(row, count), :] = pieces[step][...]
    y_rows = full[:, : 2 * B]
    rows = split(y_rows)
    out_rows[0] = rows[0]
    out_rows[1] = rows[1]
    tri = split(full[:, 2 * B :])
    out_tri[0] = tri[0]
    out_tri[1] = tri[1]
    turned = split(y_rows.T)
    out_y[0] = turned[0]
    out_y[1] = turned[1]
    y_top = (turned[0][:B], turned[1][:B])
    for copy in copies:
        copy.wait()
    leaf_top(buf[...], (rows, y_top, tri), out_mine, out_send, out_z, core, width)


def leaf_second(start, width, slab, rows, y, tri, out_mine, out_send, out_z, buf, sem):
    copies = load(slab, buf, sem, start, width)
    for copy in copies:
        copy.start()
    for copy in copies:
        copy.wait()
    mats = ((rows[0], rows[1]), (y[0, :B], y[1, :B]), (tri[0], tri[1]))
    leaf_top(buf[...], mats, out_mine, out_send, out_z, core_index(), width)


def leaf_bottom(slab, y, *refs):
    count = len(CHUNKS)
    scaled, (out, buf, result, sem) = refs[:count], refs[count:]
    get = pltpu.make_async_copy(slab.at[pl.ds(B, B), :], buf, sem.at[0])
    get.start()
    get.wait()
    low = (y[0, B:], y[1, B:])
    for (start, size), z in zip(CHUNKS, scaled):
        change = dot3(low, (z[0], z[1]))
        for side in range(2):
            at = side * HALF + start
            result[:, at : at + size] = buf[:, at : at + size] - change[:, side * size : (side + 1) * size]
    put = pltpu.make_async_copy(result, out.at[pl.ds(B, B), :], sem.at[1])
    put.start()
    put.wait()


def keep(out, place, pair):
    out[place] = pair[0]
    out[place + 1] = pair[1]


def prepare_first(own_y, own_t, other_y, other_t, out):
    keep(out, 0, split(own_y[0].T))
    keep(out, 2, split(other_y[0].T))
    keep(out, 4, split(own_y[0]))
    keep(out, 6, split(other_y[0]))
    keep(out, 8, split(jnp.where(core_index() == 0, own_t[0], other_t[0]).T))


def prepare(section, own_y, other_y, out):
    vectors = jnp.where(core_index() == 0, own_y[0], other_y[section])
    keep(out, 0, split(vectors.T))
    keep(out, 2, split(vectors))


def prepare_factors(first, own_t, other_t, got, sent, out):
    upper = got[...] + sent[...]
    for number in range(2):
        own = jnp.where(core_index() == 0, own_t[first + number], other_t[first + number])
        keep(out, 2 * number, split(jnp.where(is_low(first + number), own, upper).T))


def section_first(mine, theirs, mats, following, out_rest, out_done, out_part):
    at = lambda place: (mats[place], mats[place + 1])
    own, other = mine[...], theirs[...]
    node = dot3(at(0), split(own)) + dot3(at(2), split(other))
    node = split(dot3(at(8), split(node)))
    own = own - dot3(at(4), node)
    other = other - dot3(at(6), node)
    rest = jnp.where(core_index() == 0, own, other)
    out_rest[...] = rest
    out_done[...] = jnp.where(core_index() == 0, other, own)
    out_part[...] = dot3((following[0], following[1]), split(rest))


def update(section, part, other, rest, mats, factor):
    at = 2 * (1 - section % 2)
    node = dot3((factor[at], factor[at + 1]), split(part[...] + other[...]))
    change = dot3((mats[2], mats[3]), split(node))
    return rest[...] - jnp.where(is_member(section), change, 0.0)


def section_next(section, part, other, rest, mats, factor, following, out_rest, out_part):
    new = update(section, part, other, rest, mats, factor)
    out_rest[...] = new
    out_part[...] = dot3((following[0], following[1]), split(new))


def section_last(section, part, other, rest, mats, factor, done, out_keep, out_send):
    new = update(section, part, other, rest, mats, factor)
    out_keep[...] = jnp.where(core_index() == 0, new, done[...])
    out_send[...] = jnp.where(core_index() == 0, done[...], new)


def finish(number, kept, got, _, out, sem):
    start, size = CHUNKS[number]
    for core in range(2):

        @pl.when(core_index() == core)
        def _():
            copies = []
            for kind, (side, source) in enumerate(((core, kept), (1 - core, got))):
                place = out.at[pl.ds(0, B), pl.ds(side * HALF + start, size)]
                copies.append(pltpu.make_async_copy(source, place, sem.at[kind]))
            for copy in copies:
                copy.start()
            for copy in copies:
                copy.wait()


def ring(block, step):
    return lax.ppermute(block, "col", [(i, (i + step) % COLS) for i in range(COLS)])


def pieces_of(own):
    two_below = ring(own, 2)
    two_above = ring(own, -2)
    from_below = ring(own, 1)
    from_above = ring(own, -1)
    opposite = ring(two_below, 2)
    three_below = ring(two_below, 1)
    three_above = ring(two_above, -1)
    return [own, from_above, two_above, three_above, opposite, three_below, two_below, from_below]


def pairs(section):
    stride = 2**section
    return [
        (low, low + stride)
        for base in range(0, ROWS, 2 * stride)
        for low in ((base, base + 1) if section else (base,))
    ]


def both(routes):
    return routes + [(high, low) for low, high in routes]


def call(body, outs, specs, args, scratch=(), flops=10**9, **options):
    return pl.pallas_call(
        body,
        out_shape=outs,
        in_specs=specs,
        out_specs=jax.tree.map(lambda _: HBM if options.get("far") else VMEM, outs),
        scratch_shapes=scratch,
        compiler_params=PARAMS,
        cost_estimate=cost(flops, 3 * 10**6),
        **{key: value for key, value in options.items() if key != "far"},
    )(*args)


def swap(block, routes):
    return lax.ppermute(block, "row", routes)


def shards(slab, leaf_y, leaf_t, tree_y, tree_t):
    core = core_index()
    core_pairs = both(pairs(0))

    pieces = pieces_of(jnp.concatenate([leaf_y.T, leaf_t.T], axis=1))
    other_y = swap(tree_y, core_pairs)
    other_t = swap(tree_t, core_pairs)

    def prepared(body, count, section, own, others):
        block = pl.BlockSpec((1, B, B), lambda i: (section, 0, 0))
        return pl.pallas_call(
            body,
            grid=(1,),
            out_shape=near((count, B, B), BF16),
            in_specs=[block] * len(own) + [VMEM] * len(others),
            out_specs=VMEM,
            compiler_params=PARAMS,
            cost_estimate=cost(2 * 10**8, 2 * 10**6),
        )(*away(*own), *here(*others))

    mats = [prepared(prepare_first, 10, 0, (tree_y, tree_t), (other_y, other_t))]
    for section in range(1, LAST + 1):
        body = functools.partial(prepare, section)
        mats.append(prepared(body, 4, section, (tree_y,), (other_y,)))
    factors = [None]
    for first in (1, 3):
        block = jnp.where(core == 0, tree_t[first], other_t[first + 1])
        routes = [(low, high) for low, high in pairs(first) if low % 2 == 0]
        routes += [(low, high) for low, high in pairs(first + 1) if low % 2 == 1]
        got = swap(block, routes)
        sent = swap(got, core_pairs)
        both_factors = call(
            functools.partial(prepare_factors, first),
            near((4, B, B), BF16),
            [VMEM] * 4,
            here(tree_t, other_t, got, sent),
        )
        factors += [both_factors] * 2

    rows = slab.shape[0]
    state, scaled = [], []
    for number, (start, size) in enumerate(CHUNKS):
        outs = (near((B, size)), near((B, size)), near((2, B, 2 * size), BF16))
        scratch = [pltpu.VMEM((rows, 2 * size), F32), pltpu.SemaphoreType.DMA((2,))]
        if number == 0:
            outs += (near((2, B, rows), BF16), near((2, rows, B), BF16), near((2, B, B), BF16))
            mine, send, z, y_rows, y_cols, tri = call(
                functools.partial(leaf_first, start, size),
                outs,
                [VMEM] * COLS + [HBM],
                here(*pieces) + away(slab),
                scratch[:1] + [pltpu.VMEM((B, rows + B), F32)] + scratch[1:],
            )
        else:
            mine, send, z = call(
                functools.partial(leaf_second, start, size),
                outs,
                [HBM] + [VMEM] * 3,
                away(slab) + here(y_rows, y_cols, tri),
                scratch,
            )
        scaled.append(z)
        theirs = swap(send, core_pairs)
        state.append(
            call(section_first, (near((B, size)),) * 3, [VMEM] * 4, here(mine, theirs, mats[0], mats[1]))
        )
    result = call(
        leaf_bottom,
        struct(slab.shape),
        [HBM] + [VMEM] * (1 + len(CHUNKS)),
        away(slab) + here(y_cols, *scaled),
        [pltpu.VMEM((B, 2 * HALF), F32)] * 2 + [pltpu.SemaphoreType.DMA((2,))],
        far=True,
    )
    for section in range(1, LAST + 1):
        last = section == LAST
        for number, (_, size) in enumerate(CHUNKS):
            rest, done, part = state[number]
            other = swap(part, both(pairs(section)))
            one, two = call(
                functools.partial(section_last if last else section_next, section),
                (near((B, size)),) * 2,
                [VMEM] * 6,
                here(part, other, rest, mats[section], factors[section], done if last else mats[section + 1]),
            )
            state[number] = (one, done, two)
    got = [swap(entry[2], core_pairs) for entry in state]
    for number, entry in enumerate(state):
        result = call(
            functools.partial(finish, number),
            struct(slab.shape),
            [VMEM] * 2 + [HBM],
            here(entry[0], got[number]) + (result,),
            [pltpu.SemaphoreType.DMA((2,))],
            far=True,
            input_output_aliases={2: 0},
        )
    return result


def solution(mesh):
    in_specs = (
        P("row", "col"),
        P("row", "col"),
        P("row", "col"),
        P(None, "row", None),
        P(None, "row", None),
    )
    out_specs = P("row", "col")

    return jax.shard_map(shards, mesh=mesh, in_specs=in_specs, out_specs=out_specs, check_vma=False)
```
